256 devices in a mesh: item: 64 (over z, y, core), dp: 4 (over x).
Axes of the slice: x: 4, y: 4, z: 8, core: 2. Of those that a mesh axis runs over, the one named last changes fastest.
Arguments:
- query_feats: bfloat16 [4, 1024, 256], P('dp', 'item'), may hold values from -6 to 6
- positives: int32 [4, 1024], P('dp'), may hold values from 0 to 262143
- query_count: int32 [4, 64], P('dp'), may hold values from 1 to 16, as said below
- item_table: bfloat16 [262144, 256], P('item'), may hold values from -6 to 6
- item_gates: float32 [4, 262144], P(None, 'item'), may hold values from -5 to 5
- w_in: bfloat16 [256, 512], replicated, may hold values from -0.375 to 0.375
- w_out: bfloat16 [512, 256], replicated, may hold values from -0.25 to 0.25
- w_gate: bfloat16 [512, 4], replicated, may hold values from -1.25 to 1.25
Outputs:
- grad_feats: float32 [4, 1024, 256], P('dp', 'item')
- grad_w_in: float32 [256, 512], replicated
- grad_w_out: float32 [512, 256], replicated
- grad_w_gate: float32 [512, 4], replicated
The draws below stay inside these ranges and needn't reach their ends.
Inputs may be any that keep to these rules, and one draw needn't show every extreme that they name: `query_count`: valid queries of a device's slots; the counts of one group sum to at most 768, exactly that in some group, and some device of every group has all 16 slots valid.
All inputs are finite; a program needn't handle non-finite values.
Results may differ from the reference program's by a relative error of at most 0.0053.
Values may be sent and summed in bfloat16 or wider, within the bound.
A program may use at most 64 MiB of HBM per device.

```python
import jax
import jax.numpy as jnp
from jax import lax

DU = 256
HID = 512
EMB = 256
COMP = 4
Q_DEV = 16
ITEM_DEV = 4096
GROUPS = 4
SHARDS = 64
GROUP_SLOTS = 1024
GROUP_MOST = 768
ITEMS = 262144


def draw_query_count(key, part):
    extra_slots = Q_DEV - 1
    spare_slots = SHARDS * extra_slots
    key_group, key_total, key_full, key_perm = jax.random.split(key, 4)
    full_group = jax.random.randint(key_group, (), 0, GROUPS)
    group_totals = jax.random.randint(key_total, (GROUPS,), SHARDS + extra_slots, GROUP_MOST + 1)
    group_totals = jnp.where(jnp.arange(GROUPS, dtype=jnp.int32) == full_group, GROUP_MOST, group_totals)
    full_device = jax.random.randint(key_full, (GROUPS,), 0, SHARDS)

    def fill_group(group_key, target_total, device_full):
        permuted = jax.random.permutation(group_key, spare_slots).astype(jnp.int32)
        owner = jnp.arange(spare_slots, dtype=jnp.int32) // extra_slots
        rank_key = permuted + jnp.where(owner == device_full, 0, spare_slots)
        order = jnp.argsort(rank_key, stable=True)
        ranking = jnp.argsort(order, stable=True)
        chosen = (ranking < target_total - SHARDS).astype(jnp.int32)
        return 1 + jnp.sum(chosen.reshape(SHARDS, extra_slots), axis=1)
    group_keys = jax.random.split(key_perm, GROUPS)
    return jax.vmap(fill_group)(group_keys, group_totals, full_device).astype(jnp.int32)


def set_ends(entries, key, least, top_value):
    index_at = [jax.random.randint(jax.random.fold_in(key, axis), (), 0, length) for axis, length in enumerate(entries.shape)]
    widest = entries.shape.index(max(entries.shape))
    beside = index_at[:widest] + [(index_at[widest] + 1) % entries.shape[widest]] + index_at[widest + 1:]
    return entries.at[tuple(index_at)].set(least).at[tuple(beside)].set(top_value)


def block_scale(stream_key, extent, cuts, smallest, largest):
    def one(axis_at, shards_of):
        draws = jax.random.uniform(jax.random.fold_in(jax.random.fold_in(stream_key, 6), axis_at), (shards_of,), jnp.float32, smallest / len(cuts), largest / len(cuts))
        return jnp.repeat(jnp.exp(draws), extent[axis_at] // shards_of).reshape((-1,) + (1,) * (len(extent) - axis_at - 1))

    level = one(*cuts[0])
    for cut in cuts[1:]:
        level = level * one(*cut)
    return level


def bell_draw(key, extent, width, limit, shards=(), kind=jnp.bfloat16):
    result = width * jax.random.normal(key, extent, jnp.float32)
    if shards:
        result = result * block_scale(key, extent, shards, -0.22, 0.18)
    return jnp.clip(result, -limit, limit).astype(kind)


def setup_inputs(seed: int = 0) -> dict:
    key_of = jax.random.split(jax.random.key(seed), 9)
    return {
        "query_feats": bell_draw(key_of[0], (GROUPS, GROUP_SLOTS, DU), 1.0, 6.0, ((0, 4), (1, 64))),
        "positives": set_ends(jax.random.randint(key_of[1], (GROUPS, GROUP_SLOTS), 0, ITEMS), jax.random.fold_in(key_of[1], 1), 0, ITEMS - 1).astype(jnp.int32),
        "query_count": draw_query_count(jax.random.fold_in(key_of[8], 71), 0),
        "item_table": bell_draw(key_of[3], (ITEMS, EMB), 1.0, 6.0, ((0, 64),)),
        "item_gates": bell_draw(key_of[4], (COMP, ITEMS), 1.0, 5.0, ((1, 64),), jnp.float32),
        "w_in": bell_draw(key_of[5], (DU, HID), DU ** -0.5, 0.375),
        "w_out": bell_draw(key_of[6], (HID, EMB), HID ** -0.5, 0.25),
        "w_gate": bell_draw(key_of[7], (HID, COMP), (2.0 * HID ** -0.5), 1.25),
    }


EPS = 1e-06
TAU = 0.05

def unit_rows(raw_vals):
    scale = lax.rsqrt(lax.optimization_barrier(jnp.sum(raw_vals * raw_vals, axis=-1, keepdims=True)) + EPS)
    return (raw_vals * scale, scale)

def gate_weights(gate_logits, reduce_axis):
    exp_terms = jnp.exp(gate_logits)
    return exp_terms / lax.optimization_barrier(jnp.sum(exp_terms, axis=reduce_axis, keepdims=True))

def reference(query_feats, positives, query_count, item_table, item_gates, w_in, w_out, w_gate):
    row_total = GROUPS * GROUP_SLOTS
    comp_width = EMB // COMP
    features = query_feats.reshape(row_total, DU)
    slot_index = jnp.arange(GROUP_SLOTS, dtype=jnp.int32)
    valid_slot = ((slot_index % Q_DEV)[None, :] < query_count[:, slot_index // Q_DEV]).reshape(row_total)
    valid_f = valid_slot.astype(jnp.float32)
    positive = positives.reshape(row_total)
    preact = jnp.dot(features, w_in, preferred_element_type=jnp.float32)
    hidden = jax.nn.silu(preact).astype(jnp.bfloat16)
    query_raw = jnp.dot(hidden, w_out, preferred_element_type=jnp.float32).reshape(row_total, COMP, comp_width)
    query_gate = jnp.dot(hidden, w_gate, preferred_element_type=jnp.float32).astype(jnp.bfloat16)
    query_unit, query_scale = unit_rows(query_raw)
    query_norm = query_unit.astype(jnp.bfloat16)
    item_raw = item_table.astype(jnp.float32).reshape(ITEMS, COMP, comp_width)
    item_norm = unit_rows(item_raw)[0].astype(jnp.bfloat16)
    block_len = min(512, ITEM_DEV)
    block_count = ITEMS // block_len
    item_blocks = item_norm.reshape(block_count, block_len, COMP, comp_width)
    gate_blocks = item_gates.T.reshape(block_count, block_len, COMP)
    query_float_rows = query_norm.astype(jnp.float32)
    gate_f = query_gate.astype(jnp.float32)

    def one_block(state_in, input_block_part):
        totals, update_delta, gate_sum = state_in
        item_part, gate_part = input_block_part
        item_float_rows = item_part.astype(jnp.float32)
        score_matrix = jnp.einsum('cnt,ent->cen', query_float_rows, item_float_rows)
        weights = gate_weights(gate_f[:, None, :] + gate_part[None, :, :], 2)
        logits = lax.optimization_barrier(jnp.sum(weights * score_matrix, axis=-1)) / TAU
        exp_logit = jnp.exp(logits)
        totals = totals + lax.optimization_barrier(jnp.sum(exp_logit, axis=1))
        coef_bf = (exp_logit[:, :, None] * weights / TAU).astype(jnp.bfloat16)
        coefficient_float = lax.optimization_barrier(coef_bf).astype(jnp.float32)
        update_delta = update_delta + jnp.einsum('ezt,ztu->etu', coefficient_float, item_float_rows)
        gate_sum = gate_sum + lax.optimization_barrier(jnp.sum(exp_logit[:, :, None] * weights * (score_matrix - TAU * logits[:, :, None]), axis=1)) / TAU
        return ((totals, update_delta, gate_sum), None)
    initial = (jnp.zeros((row_total,), jnp.float32), jnp.zeros((row_total, COMP, comp_width), jnp.float32), jnp.zeros((row_total, COMP), jnp.float32))
    (totals, update_delta, gate_sum), _ = lax.scan(one_block, initial, (item_blocks, gate_blocks))
    item_pos = item_norm[positive].astype(jnp.float32)
    score_pos = lax.optimization_barrier(jnp.sum(query_float_rows * item_pos, axis=-1))
    weight_pos = gate_weights(gate_f + item_gates[:, positive].T, 1)
    logit_pos = lax.optimization_barrier(jnp.sum(weight_pos * score_pos, axis=-1)) / TAU
    pos_query = weight_pos[:, :, None] * item_pos / TAU
    pos_gate = weight_pos * (score_pos - TAU * logit_pos[:, None]) / TAU
    grad_query = (update_delta / totals[:, None, None] - pos_query) * valid_f[:, None, None]
    grad_gate = (gate_sum / totals[:, None] - pos_gate) * valid_f[:, None]
    dot_sum = lax.optimization_barrier(jnp.sum(grad_query * query_raw, axis=-1, keepdims=True))
    grad_raw = (query_scale * grad_query - query_raw * query_scale ** 3 * dot_sum).reshape(row_total, EMB)
    highest = lax.Precision.HIGHEST
    grad_hidden = jnp.dot(grad_raw, w_out.astype(jnp.float32).T, precision=highest) + jnp.dot(grad_gate, w_gate.astype(jnp.float32).T, precision=highest)
    sigmoid_pre = jax.nn.sigmoid(preact)
    grad_preact = grad_hidden * sigmoid_pre * (1.0 + preact * (1.0 - sigmoid_pre))
    grad_feats = jnp.dot(grad_preact, w_in.astype(jnp.float32).T, precision=highest).reshape(GROUPS, GROUP_SLOTS, DU)
    hidden_f = hidden.astype(jnp.float32)
    grad_w_in = jnp.dot(features.astype(jnp.float32).T, grad_preact, precision=highest)
    grad_w_out = jnp.dot(hidden_f.T, grad_raw, precision=highest)
    grad_w_gate = jnp.dot(hidden_f.T, grad_gate, precision=highest)
    return (grad_feats, grad_w_in, grad_w_out, grad_w_gate)
```

```python
import functools
import math

import jax
import jax.numpy as jnp
from jax import lax
from jax.experimental import pallas as pl
from jax.experimental.pallas import tpu as pltpu
from jax.sharding import PartitionSpec as P

EPS = 1e-06
TAU = 0.05
LOG2E = math.log2(math.e)
LN2 = math.log(2.0)
LANES = 128
CHUNK = 24
PAY = 56
F32 = jnp.float32
BF16 = jnp.bfloat16
MESH = pl.DeviceIdType.MESH


def mm(a, b):
    return lax.dot_general(a, b, (((1,), (0,)), ((), ())), preferred_element_type=F32)


def mm_nt(a, b):
    return lax.dot_general(a, b, (((1,), (1,)), ((), ())), preferred_element_type=F32)


def mm_tn(a, b):
    return lax.dot_general(a, b, (((0,), (0,)), ((), ())), preferred_element_type=F32)


def parts(x, n):
    out = []
    for step in range(n):
        hi = x.astype(BF16)
        out.append(hi)
        if step < n - 1:
            x = x - hi.astype(F32)
    return out


def mmx(x, b, n):
    total = None
    for part in parts(x, n):
        prod = mm(part, b)
        total = prod if total is None else total + prod
    return total


def iota(shape, dim):
    return lax.broadcasted_iota(jnp.int32, shape, dim)


def onehot(cond):
    return jnp.where(cond, 1.0, 0.0).astype(BF16)


def comp_spread(rows, comps, width):
    per = width // comps
    shape = (rows, width)
    return onehot(iota(shape, 0) == iota(shape, 1) // per)


def comp_fold(width, comps):
    per = width // comps
    shape = (width, LANES)
    return onehot(iota(shape, 0) // per == iota(shape, 1))


def comp_block(width, comps):
    per = width // comps
    shape = (width, width)
    return onehot(iota(shape, 0) // per == iota(shape, 1) // per)


def place(n_y, n_z):
    me = lax.axis_index("item")
    core = lax.rem(me, 2)
    y = lax.rem(me // 2, n_y)
    z = me // (2 * n_y)
    return core, y, z


def item_id(core, y, z, n_y):
    return (z * n_y + y) * 2 + core


def remote(src, dst, send, recv, item, dp):
    return pltpu.make_async_remote_copy(
        src_ref=src,
        dst_ref=dst,
        send_sem=send,
        recv_sem=recv,
        device_id=(item, dp),
        device_id_type=MESH,
    )


def greet(peers):
    barrier = pltpu.get_barrier_semaphore()
    for item, dp in peers:
        pl.semaphore_signal(barrier, inc=1, device_id=(item, dp), device_id_type=MESH)
    pl.semaphore_wait(barrier, len(peers))


def item_peers(core, y, z, n_y, n_z, dp):
    z_peers = [(item_id(core, y, lax.rem(z + s, n_z), n_y), dp) for s in range(1, n_z)]
    y_peers = [(item_id(core, lax.rem(y + s, n_y), z, n_y), dp) for s in range(1, n_y)]
    partner = (item_id(1 - core, y, z, n_y), dp)
    return z_peers, y_peers, partner


def spread_blocks(buf, core, y, z, peers, sems):
    z_peers, y_peers, partner = peers
    zs, zr, ys, yr, cs, cr = sems
    copies = []
    for s, (item, dp) in enumerate(z_peers):
        block = buf.at[core, y, z]
        copies.append(remote(block, block, zs.at[s], zr.at[s], item, dp))
        copies[-1].start()
    for copy in copies:
        copy.wait()
    copies = []
    for s, (item, dp) in enumerate(y_peers):
        block = buf.at[core, y]
        copies.append(remote(block, block, ys.at[s], yr.at[s], item, dp))
        copies[-1].start()
    for copy in copies:
        copy.wait()
    block = buf.at[core]
    copy = remote(block, block, cs, cr, partner[0], partner[1])
    copy.start()
    copy.wait()


def gather_sems(n_y, n_z):
    dma = pltpu.SemaphoreType.DMA
    return [dma((n_z - 1,)), dma((n_z - 1,)), dma((n_y - 1,)), dma((n_y - 1,)), dma(()), dma(())]


def gather_kernel(n_y, n_z, x_ref, o_ref, local_sem, *sems):
    core, y, z = place(n_y, n_z)
    dp = lax.axis_index("dp")
    peers = item_peers(core, y, z, n_y, n_z, dp)
    mine = pltpu.make_async_copy(x_ref, o_ref.at[core, y, z], local_sem)
    mine.start()
    greet(peers[0] + peers[1] + [peers[2]])
    mine.wait()
    spread_blocks(o_ref, core, y, z, peers, sems)


def gather_rows(x, n_y, n_z):
    return pl.pallas_call(
        functools.partial(gather_kernel, n_y, n_z),
        out_shape=jax.ShapeDtypeStruct((2, n_y, n_z) + x.shape, x.dtype),
        in_specs=[pl.BlockSpec(memory_space=pltpu.VMEM)],
        out_specs=pl.BlockSpec(memory_space=pltpu.VMEM),
        scratch_shapes=[pltpu.SemaphoreType.DMA(())] + gather_sems(n_y, n_z),
        compiler_params=pltpu.CompilerParams(collective_id=0, has_side_effects=True),
        name="gather_rows",
    )(x)


def query_tower(x, w_in, w_out, w_gate):
    pre = mm(x, w_in)
    hid = (pre * jax.nn.sigmoid(pre)).astype(BF16)
    raw = mm(hid, w_out)
    gate = mm(hid, w_gate).astype(BF16).astype(F32)
    return pre, hid, raw, gate


def sweep_kernel(
    comps,
    x_ref,
    rank_ref,
    pos_ref,
    tab_ref,
    gate_ref,
    w_in_ref,
    w_out_ref,
    w_gate_ref,
    pay_ref,
    qb_ref,
    xc_ref,
    pre_ref,
    hid_ref,
    raw_ref,
    scaled_ref,
    normed_ref,
    ei_den,
    ei_sum,
    q_ref,
    qn_ref,
    eq_ref,
    eqb_ref,
    posc_ref,
    acc,
    pos_acc,
    tot_acc,
    g_acc,
    p_acc,
    sc_ref,
):
    rows, emb = q_ref.shape
    items = tab_ref.shape[0]
    slots = x_ref.shape[0]
    rb = 256 if rows % 256 == 0 else rows
    it = 512 if items % 512 == 0 else items
    spread = comp_spread(LANES, comps, emb)
    fold = comp_fold(emb, comps)
    block = comp_block(emb, comps)
    lane_shape = (rb, LANES)
    is_comp = iota(lane_shape, 1) < comps

    spread16 = onehot(
        (iota((16, emb), 0) % 4 == iota((16, emb), 1) // (emb // comps)) & (iota((16, emb), 0) < 12)
    )

    @pl.loop(0, items // it)
    def _(t):
        sl = pl.ds(pl.multiple_of(t * it, it), it)
        tab = tab_ref[sl, :].astype(F32)
        norm = (tab * lax.rsqrt(mmx(tab * tab, block, 2) + EPS)).astype(BF16)
        normed_ref[sl, :] = norm
        ei = jnp.exp(gate_ref[:, sl])
        hi, lo, lo2 = parts(ei, 3)
        row = iota(ei.shape, 0)
        zero = jnp.zeros_like(ei)
        hi, lo, lo2 = hi.astype(F32), lo.astype(F32), lo2.astype(F32)
        ei_den[:, sl] = jnp.where(row < 8, hi, jnp.where(row < 12, lo, zero)).astype(BF16)
        ei_sum[:, sl] = jnp.where(row < 4, hi, jnp.where(row < 8, lo, zero)).astype(BF16)
        ei_all = jnp.where(row < 4, hi, jnp.where(row < 8, lo, jnp.where(row < 12, lo2, zero))).astype(BF16)
        factor = mm_tn(ei_all, spread16)
        scaled_ref[sl, :] = (norm.astype(F32) * factor).astype(BF16)

    shift_a = onehot(
        ((iota((LANES, 16), 1) == iota((LANES, 16), 0)) | (iota((LANES, 16), 1) == iota((LANES, 16), 0) + 8))
        & (iota((LANES, 16), 0) < 4)
    )
    shift_b = onehot((iota((LANES, 16), 1) == iota((LANES, 16), 0) + 4) & (iota((LANES, 16), 0) < 4))
    for r in range(rows // rb):
        rs = slice(r * rb, (r + 1) * rb)
        picked = iota((rb, slots), 0) + r * rb == rank_ref[...]
        xc = mm(onehot(picked), x_ref[...]).astype(BF16)
        posc_ref[rs, :] = jnp.sum(jnp.where(picked, pos_ref[...], 0.0), axis=1, keepdims=True)
        pre, hid, raw, gate = query_tower(xc, w_in_ref[...], w_out_ref[...], w_gate_ref[...])
        xc_ref[rs, :] = xc
        pre_ref[rs, :] = pre
        hid_ref[rs, :] = hid
        raw_ref[rs, :] = raw
        qn = (raw * lax.rsqrt(mmx(raw * raw, block, 3) + EPS)).astype(BF16)
        qn_ref[rs, :] = qn
        top = jnp.max(jnp.where(is_comp, gate, -3.0e38), axis=1, keepdims=True)
        eq = jnp.where(is_comp, jnp.exp(gate - top), 0.0)
        eqb = mmx(eq, spread, 3)
        eqb_ref[rs, :] = eqb
        q_ref[rs, :] = (qn.astype(F32) * (eqb * (LOG2E / TAU))).astype(BF16)
        hi, lo = parts(eq, 2)
        eq_ref[rs, :] = (mm(hi, shift_a) + mm(lo, shift_b)).astype(BF16)

    acc[...] = jnp.zeros_like(acc)
    pos_acc[...] = jnp.zeros_like(pos_acc)
    tot_acc[...] = jnp.zeros_like(tot_acc)
    g_acc[...] = jnp.zeros_like(g_acc)
    p_acc[...] = jnp.zeros_like(p_acc)

    @pl.loop(0, items // it)
    def _(t):
        sl = pl.ds(pl.multiple_of(t * it, it), it)
        local = iota((rb, it), 1) + t * it
        for r in range(rows // rb):
            rs = slice(r * rb, (r + 1) * rb)
            num = mm_nt(q_ref[rs, :], scaled_ref[sl, :])
            den = mm(eq_ref[rs, :], ei_den[:, sl])
            inv = 1.0 / den
            log2_expo = num * inv
            expo = jnp.exp2(log2_expo)
            coef = expo * inv
            tot_acc[rs, :] += jnp.sum(expo, axis=1, keepdims=True)
            acc[rs, :] += mm(coef.astype(BF16), scaled_ref[sl, :])
            g_acc[rs, :] += mm_nt((coef * log2_expo).astype(BF16), ei_sum[:, sl])
            here = onehot(posc_ref[rs, :].astype(jnp.int32) == local)
            pos_acc[rs, :] += mm(here, normed_ref[sl, :])
            p_acc[rs, :] += mm_nt(here, ei_sum[:, sl])

    fold16 = onehot((iota((16, LANES), 0) % 4 == iota((16, LANES), 1)) & (iota((16, LANES), 0) < 8))
    ll = (LANES, LANES)
    spot = 8 * (iota(ll, 0) // 2) + iota(ll, 0) % 2
    to_g, to_hi, to_lo = (onehot((iota(ll, 1) == spot + j) & (iota(ll, 0) < comps)) for j in (2, 4, 6))
    lane = iota(lane_shape, 1)
    for r in range(rows // rb):
        rs = slice(r * rb, (r + 1) * rb)
        eqb = eqb_ref[rs, :]
        acc[rs, :] = acc[rs, :] * eqb * (1.0 / TAU)
        eq = mmx(eq_ref[rs, :].astype(F32), fold16, 1)
        second = eq * mmx(g_acc[rs, :], fold16, 3) * LN2
        weight = eq * mmx(p_acc[rs, :], fold16, 3)
        weight_sum = jnp.sum(weight, axis=1, keepdims=True)
        weight = weight / jnp.where(weight_sum > 0.0, weight_sum, 1.0)
        pos_item = pos_acc[rs, :]
        score = mmx(qn_ref[rs, :].astype(F32) * pos_item, fold, 3)
        logit = jnp.sum(weight * score, axis=1, keepdims=True) / TAU
        pos_acc[rs, :] = mmx(weight, spread, 3) * pos_item * (1.0 / TAU)
        tot_hi, tot_lo = parts(tot_acc[rs, :], 2)
        scalars = jnp.where(lane % 8 == 0, tot_hi.astype(F32), jnp.where(lane % 8 == 1, tot_lo.astype(F32), 0.0))
        pg_hi, pg_lo = parts(weight * (score * (1.0 / TAU) - logit), 2)
        scalars = scalars + mmx(second, to_g, 1) + mm(pg_hi, to_hi) + mm(pg_lo, to_lo)
        sc_ref[rs, :] = scalars.astype(BF16)
    sc_ref[rows:, :] = jnp.zeros((LANES, LANES), BF16)

    n_y, n_z = pay_ref.shape[1:3]
    eye = onehot(iota((16, LANES), 0) == iota((16, LANES), 1))
    for b in range(n_y * n_z):
        y, z = b // n_z, b % n_z
        rs = slice(b * CHUNK, (b + 1) * CHUNK)
        scalars = mm_nt(eye, sc_ref[b * CHUNK : b * CHUNK + LANES, :])
        for c in range(2):
            cols = slice(c * LANES, (c + 1) * LANES)
            pay_ref[c, y, z, 0:CHUNK, :] = acc[rs, cols].astype(BF16)
            pay_ref[c, y, z, CHUNK : 2 * CHUNK, :] = pos_acc[rs, cols].astype(BF16)
            pay_ref[c, y, z, 2 * CHUNK : PAY, :] = scalars[c * 8 : c * 8 + 8, :].astype(BF16)
            qb_ref[c, y, z] = qn_ref[rs, cols]


def sweep(x_all, ranks, pos_local, table, gates16, w_in, w_out, w_gate, comps, rows, n_y, n_z):
    emb, hid = w_out.shape[1], w_out.shape[0]
    items = table.shape[0]
    vmem = pl.BlockSpec(memory_space=pltpu.VMEM)
    sds = jax.ShapeDtypeStruct
    return pl.pallas_call(
        functools.partial(sweep_kernel, comps),
        out_shape=(
            sds((2, n_y, n_z, PAY, LANES), BF16),
            sds((2, n_y, n_z, CHUNK, LANES), BF16),
            sds((rows, x_all.shape[1]), BF16),
            sds((rows, hid), F32),
            sds((rows, hid), BF16),
            sds((rows, emb), F32),
        ),
        in_specs=[vmem] * 8,
        out_specs=(vmem,) * 6,
        scratch_shapes=[
            pltpu.VMEM((items, emb), BF16),
            pltpu.VMEM((items, emb), BF16),
            pltpu.VMEM((16, items), BF16),
            pltpu.VMEM((16, items), BF16),
            pltpu.VMEM((rows, emb), BF16),
            pltpu.VMEM((rows, emb), BF16),
            pltpu.VMEM((rows, 16), BF16),
            pltpu.VMEM((rows, emb), F32),
            pltpu.VMEM((rows, 1), F32),
            pltpu.VMEM((rows, emb), F32),
            pltpu.VMEM((rows, emb), F32),
            pltpu.VMEM((rows, 1), F32),
            pltpu.VMEM((rows, 16), F32),
            pltpu.VMEM((rows, 16), F32),
            pltpu.VMEM((rows + LANES, LANES), BF16),
        ],
        compiler_params=pltpu.CompilerParams(vmem_limit_bytes=56 * 1024 * 1024),
        name="sweep",
    )(x_all, ranks, pos_local, table, gates16, w_in, w_out, w_gate)


def reduce_kernel(n_y, n_z, pay_ref, qb_ref, o_ref, in_c, acc_c, in_y, acc_y, in_z, *sems):
    core, y, z = place(n_y, n_z)
    dp = lax.axis_index("dp")
    peers = item_peers(core, y, z, n_y, n_z, dp)
    z_peers, y_peers, partner = peers
    cs, cr, ys, yr, zs, zr = sems[:6]
    greet(z_peers + y_peers + [partner])

    copy = remote(pay_ref.at[1 - core], in_c, cs, cr, partner[0], partner[1])
    copy.start()
    copy.wait()
    for j in range(n_y):
        acc_c[j] = (pay_ref[core, j].astype(F32) + in_c[j].astype(F32)).astype(BF16)

    copies = []
    for s, (item, _) in enumerate(y_peers):
        target = lax.rem(y + s + 1, n_y)
        copies.append(remote(acc_c.at[target], in_y.at[s], ys.at[s], yr.at[s], item, dp))
        copies[-1].start()
    for copy in copies:
        copy.wait()
    total = acc_c[y].astype(F32)
    for s in range(n_y - 1):
        total = total + in_y[s].astype(F32)
    acc_y[...] = total.astype(BF16)

    copies = []
    for s, (item, _) in enumerate(z_peers):
        target = lax.rem(z + s + 1, n_z)
        copies.append(remote(acc_y.at[target], in_z.at[s], zs.at[s], zr.at[s], item, dp))
        copies[-1].start()
    for copy in copies:
        copy.wait()
    total = acc_y[z].astype(F32)
    for s in range(n_z - 1):
        total = total + in_z[s].astype(F32)

    update, positive, scal = total[0:CHUNK], total[CHUNK : 2 * CHUNK], total[2 * CHUNK : PAY]
    lane = iota((8, LANES), 1)
    row = iota((8, LANES), 0)
    soft_row = jnp.where(lane[0:1] < CHUNK, scal[0:1] + scal[1:2], 1.0)
    diag = iota((CHUNK, LANES), 0) == iota((CHUNK, LANES), 1)
    soft_col = jnp.sum(jnp.where(diag, soft_row, 0.0), axis=1, keepdims=True)
    inner = qb_ref[core, y, z].astype(F32) * update
    inner = jnp.concatenate([inner, jnp.zeros((LANES - CHUNK, LANES), F32)], axis=0)
    select = onehot(row == lane // (LANES // 2) + 2)
    first = sum(mm_nt(select, part) for part in parts(inner, 3))
    gate = (first - scal) / soft_row - pltpu.roll(scal, 6, 0) - pltpu.roll(scal, 4, 0)
    gate = jnp.where((row >= 2) & (row < 4) & (lane < CHUNK), gate, 0.0)
    hi = gate.astype(BF16).astype(F32)
    low = pltpu.roll(gate - hi, 2, 0)
    o_ref[core, y, z, 0:CHUNK, :] = (update / soft_col - positive).astype(BF16)
    o_ref[core, y, z, CHUNK : CHUNK + 8, :] = (hi + low).astype(BF16)
    spread_blocks(o_ref, core, y, z, peers, sems[6:])


def reduce_rows(pay, qb, n_y, n_z):
    vmem = pl.BlockSpec(memory_space=pltpu.VMEM)
    dma = pltpu.SemaphoreType.DMA
    block = (PAY, LANES)
    return pl.pallas_call(
        functools.partial(reduce_kernel, n_y, n_z),
        out_shape=jax.ShapeDtypeStruct((2, n_y, n_z, CHUNK + 8, LANES), BF16),
        in_specs=[vmem] * 2,
        out_specs=vmem,
        scratch_shapes=[
            pltpu.VMEM((n_y, n_z) + block, BF16),
            pltpu.VMEM((n_y, n_z) + block, BF16),
            pltpu.VMEM((n_y - 1, n_z) + block, BF16),
            pltpu.VMEM((n_z,) + block, BF16),
            pltpu.VMEM((n_z - 1,) + block, BF16),
            dma(()),
            dma(()),
            dma((n_y - 1,)),
            dma((n_y - 1,)),
            dma((n_z - 1,)),
            dma((n_z - 1,)),
        ]
        + gather_sems(n_y, n_z),
        compiler_params=pltpu.CompilerParams(
            collective_id=1, has_side_effects=True, vmem_limit_bytes=32 * 1024 * 1024
        ),
        name="reduce_rows",
    )(pay, qb)


def backward_kernel(
    comps,
    own_ref,
    g_ref,
    xc_ref,
    pre_ref,
    hid_ref,
    raw_ref,
    w_in_ref,
    w_out_ref,
    w_gate_ref,
    stack_ref,
    gate_ref,
    feats_ref,
    gq_ref,
    vv_ref,
):
    rows, emb = raw_ref.shape
    n_y, n_z = g_ref.shape[1:3]
    blocks = n_y * n_z
    for b in range(blocks):
        y, z = b // n_z, b % n_z
        for c in range(2):
            gq_ref[b * CHUNK : (b + 1) * CHUNK, c * LANES : (c + 1) * LANES] = g_ref[c, y, z, 0:CHUNK, :]
            at = (c * blocks + b) * 8
            vv_ref[at : at + 8, :] = g_ref[c, y, z, CHUNK : CHUNK + 8, :]

    width = blocks * 16
    eye = onehot(iota((32, LANES), 0) == iota((32, LANES), 1))
    spots = mm_nt(eye, vv_ref[...]).astype(BF16)
    repeat = onehot(iota((rows, 32), 0) % CHUNK == iota((rows, 32), 1))
    wide = mm(repeat, spots)
    wide = jnp.where(iota((rows, width), 0) // CHUNK == iota((rows, width), 1) // 8 % blocks, wide, 0.0).astype(BF16)
    at_w = iota((width, LANES), 0)
    lane_w = iota((width, LANES), 1) - 2 * (at_w // (8 * blocks))
    kind = at_w % 8
    collect = onehot(((kind == lane_w + 2) | (kind == lane_w + 4)) & (lane_w >= 0) & (lane_w < 2))
    gate = mm(wide, collect)

    block = comp_block(emb, comps)
    gq = gq_ref[...].astype(F32)
    raw = raw_ref[...]
    scale = lax.rsqrt(mmx(raw * raw, block, 3) + EPS)
    dot_sum = mmx(gq * raw, block, 3)
    g_raw = scale * gq - raw * (scale * scale * scale) * dot_sum
    raw_hi, raw_lo = parts(g_raw, 2)
    gate_hi, gate_lo = parts(gate, 2)
    w_out = w_out_ref[...]
    w_gate = w_gate_ref[...]
    g_hid = mm_nt(raw_hi, w_out) + mm_nt(raw_lo, w_out) + mm_nt(gate_hi, w_gate) + mm_nt(gate_lo, w_gate)
    pre = pre_ref[...]
    sig = jax.nn.sigmoid(pre)
    g_pre = g_hid * sig * (1.0 + pre * (1.0 - sig))
    pre_hi, pre_lo = parts(g_pre, 2)

    xc = xc_ref[...]
    hid = hid_ref[...]
    g_in = mm_tn(xc, pre_hi) + mm_tn(xc, pre_lo)
    feat_w = xc.shape[1]
    n_in = g_in.shape[1] // emb
    for j in range(n_in):
        stack_ref[j * feat_w : (j + 1) * feat_w, :] = g_in[:, j * emb : (j + 1) * emb].astype(BF16)
    stack_ref[n_in * feat_w :, :] = (mm_tn(hid, raw_hi) + mm_tn(hid, raw_lo)).astype(BF16)
    gate_ref[...] = (mm_tn(gate_hi, hid) + mm_tn(gate_lo, hid))[0:8, :]

    own = feats_ref.shape[0]
    slot = iota((own, rows), 0)
    take = onehot((iota((own, rows), 1) == slot + own_ref[0]) & (slot < own_ref[1]))
    mine = mm(take, pre_hi) + mm(take, pre_lo)
    feats_ref[...] = sum(mm_nt(part, w_in_ref[...]) for part in parts(mine, 3))


def backward(own, g_all, xc, pre, hid, raw, w_in, w_out, w_gate, comps, own_rows):
    vmem = pl.BlockSpec(memory_space=pltpu.VMEM)
    sds = jax.ShapeDtypeStruct
    rows, emb = raw.shape
    feat_w, hid_w = w_in.shape
    n_y, n_z = g_all.shape[1:3]
    stack_rows = feat_w * (hid_w // emb) + hid_w
    return pl.pallas_call(
        functools.partial(backward_kernel, comps),
        out_shape=(
            sds((stack_rows, emb), BF16),
            sds((8, hid_w), F32),
            sds((own_rows, feat_w), F32),
        ),
        in_specs=[pl.BlockSpec(memory_space=pltpu.SMEM)] + [vmem] * 8,
        out_specs=(vmem,) * 3,
        scratch_shapes=[pltpu.VMEM((rows, emb), BF16), pltpu.VMEM((n_y * n_z * 16, LANES), BF16)],
        compiler_params=pltpu.CompilerParams(vmem_limit_bytes=56 * 1024 * 1024),
        name="backward",
    )(own, g_all, xc, pre, hid, raw, w_in, w_out, w_gate)


def weights_kernel(n_y, n_z, n_g, stack_ref, gate_ref, in_ref, out_ref, go_ref, x_buf, g_buf, full, *sems):
    core, y, z = place(n_y, n_z)
    dp = lax.axis_index("dp")
    me = item_id(core, y, z, n_y)
    _, y_peers, partner = item_peers(core, y, z, n_y, n_z, dp)
    x_peers = [(me, lax.rem(dp + s, n_g)) for s in range(1, n_g)]
    xs, xr, gs, gr, ys, yr, cs, cr, local = sems
    greet(x_peers + y_peers + [partner])

    copies = []
    for s, (item, group) in enumerate(x_peers):
        copies.append(remote(stack_ref.at[core, y], x_buf.at[dp], xs.at[s], xr.at[s], item, group))
        copies[-1].start()
        copies.append(remote(gate_ref, g_buf.at[dp], gs.at[s], gr.at[s], item, group))
        copies[-1].start()
    mine = pltpu.make_async_copy(stack_ref.at[core, y], x_buf.at[dp], local.at[0])
    mine.start()
    mine_g = pltpu.make_async_copy(gate_ref, g_buf.at[dp], local.at[1])
    mine_g.start()
    mine.wait()
    mine_g.wait()
    for copy in copies:
        copy.wait()
    total = x_buf[0].astype(F32)
    gate = g_buf[0]
    for j in range(1, n_g):
        total = total + x_buf[j].astype(F32)
        gate = gate + g_buf[j]
    full[core, y] = total.astype(BF16)
    go_ref[...] = gate

    copies = []
    for s, (item, _) in enumerate(y_peers):
        block = full.at[core, y]
        copies.append(remote(block, block, ys.at[s], yr.at[s], item, dp))
        copies[-1].start()
    for copy in copies:
        copy.wait()
    block = full.at[core]
    copy = remote(block, block, cs, cr, partner[0], partner[1])
    copy.start()
    copy.wait()

    feat_w, hid_w = in_ref.shape
    emb = out_ref.shape[1]
    span = full.shape[2]
    n_in = feat_w * (hid_w // emb)
    for c in range(2):
        for j in range(n_y):
            at = (c * n_y + j) * span
            value = full[c, j].astype(F32)
            if at < n_in:
                col, row = at // feat_w, at % feat_w
                in_ref[row : row + span, col * emb : (col + 1) * emb] = value
            else:
                out_ref[at - n_in : at - n_in + span, :] = value


def weights(stack, gate, feat_w, hid_w, n_y, n_z, n_g):
    vmem = pl.BlockSpec(memory_space=pltpu.VMEM)
    dma = pltpu.SemaphoreType.DMA
    sds = jax.ShapeDtypeStruct
    span = stack.shape[0] // (2 * n_y)
    emb = stack.shape[1]
    return pl.pallas_call(
        functools.partial(weights_kernel, n_y, n_z, n_g),
        out_shape=(sds((feat_w, hid_w), F32), sds((hid_w, emb), F32), sds(gate.shape, F32)),
        in_specs=[vmem] * 2,
        out_specs=(vmem,) * 3,
        scratch_shapes=[
            pltpu.VMEM((n_g, span, emb), BF16),
            pltpu.VMEM((n_g,) + gate.shape, F32),
            pltpu.VMEM((2, n_y, span, emb), BF16),
            dma((n_g - 1,)),
            dma((n_g - 1,)),
            dma((n_g - 1,)),
            dma((n_g - 1,)),
            dma((n_y - 1,)),
            dma((n_y - 1,)),
            dma(()),
            dma(()),
            dma((2,)),
        ],
        compiler_params=pltpu.CompilerParams(collective_id=2, has_side_effects=True),
        name="weights",
    )(stack.reshape(2, n_y, span, emb), gate)


def per_device(n_y, n_z, n_g, query_feats, positives, query_count, item_table, item_gates, w_in, w_out, w_gate):
    shards = 2 * n_y * n_z
    own_rows, feat_w = query_feats.shape[1:]
    comps = w_gate.shape[1]
    slots = own_rows * shards
    rows = CHUNK * n_y * n_z
    items = item_table.shape[0]

    gathered = gather_rows(query_feats[0], n_y, n_z).reshape(slots, feat_w)

    def by_place(values):
        inner = values.shape[1:]
        order = (2, 1, 0) + tuple(range(3, 3 + len(inner)))
        return values.reshape((n_z, n_y, 2) + inner).transpose(order).reshape(values.shape)

    core, y, z = place(n_y, n_z)
    here = (core * n_y + y) * n_z + z
    counts = by_place(query_count[0])
    index = jnp.arange(shards, dtype=jnp.int32)
    offset = jnp.sum(jnp.where(index[:, None] < index[None, :], counts[:, None], 0), axis=0)
    slot = jnp.arange(own_rows, dtype=jnp.int32)
    ranks = jnp.where(slot[None, :] < counts[:, None], offset[:, None] + slot[None, :], -1).reshape(1, slots)
    pos_local = by_place(positives[0].reshape(shards, own_rows)).reshape(1, slots)
    pos_local = (pos_local - lax.axis_index("item") * items).astype(F32)
    own = jnp.stack(
        [jnp.sum(jnp.where(index == here, offset, 0)), jnp.sum(jnp.where(index == here, counts, 0))]
    )
    gates16 = jnp.concatenate([item_gates] * 4, axis=0)
    w_gate_wide = jnp.pad(w_gate, ((0, 0), (0, LANES - comps)))

    pay, qb, xc, pre, hid, raw = sweep(
        gathered, ranks, pos_local, item_table, gates16, w_in, w_out, w_gate_wide, comps, rows, n_y, n_z
    )
    g_all = reduce_rows(pay, qb, n_y, n_z)
    stack, gate, feats = backward(own, g_all, xc, pre, hid, raw, w_in, w_out, w_gate_wide, comps, own_rows)
    g_in, g_out, g_gate = weights(stack, gate, feat_w, w_in.shape[1], n_y, n_z, n_g)
    return feats.reshape(1, own_rows, feat_w), g_in, g_out, g_gate[:comps].T


def solution(mesh):
    shards = mesh.shape["item"]
    n_y = 4 if shards >= 64 else 2
    n_z = shards // (2 * n_y)
    in_specs = (
        P("dp", "item", None),
        P("dp", None),
        P("dp", None),
        P("item", None),
        P(None, "item"),
        P(),
        P(),
        P(),
    )
    out_specs = (P("dp", "item", None), P(), P(), P())
    return jax.shard_map(
        functools.partial(per_device, n_y, n_z, mesh.shape["dp"]),
        mesh=mesh,
        in_specs=in_specs,
        out_specs=out_specs,
        check_vma=False,
    )
```
